128 devices in a mesh: pipe: 4 (over y_lo, core), seq: 32 (over x, y_hi, z).
Axes of the slice: x: 4, y: 4 (y_hi: 2, y_lo: 2; y = y_hi * 2 + y_lo), z: 4, core: 2. Of those that a mesh axis runs over, the one named last changes fastest.
Arguments:
- queries: bfloat16 [4, 16384, 4096], P('pipe', 'seq'), may hold values from -34 to 34
- keys: bfloat16 [4, 16384, 4096], P('pipe', 'seq'), may hold values from -6 to 6
- values: bfloat16 [4, 16384, 4096], P('pipe', 'seq'), may hold values from -6 to 6
- key_blocks: int32 [4, 128, 12], P('pipe'), may hold values from 0 to 127, as said below
- key_count: int32 [4, 128], P('pipe'), may hold values from 1 to 12
Outputs:
- handed: bfloat16 [4, 16384, 4096], P('pipe', 'seq')
The draws below stay inside these ranges and needn't reach their ends.
Inputs may be any that keep to these rules, and one draw needn't show every extreme that they name: Row b of key_blocks[s] lists 12 distinct blocks; its first entry is b; every entry lies in a frame no later than b's, where the frame of a block is the block index // 32.
All inputs are finite; a program needn't handle non-finite values.
Results may differ from the reference program's by a relative error of at most 0.0045.
Values may be sent and summed in bfloat16 or wider, within the bound.
No kernel may reach another device: no remote copies, remote signals or barrier semaphores. Data moves between devices by JAX's collectives and lax.ppermute only.
A program may use at most 128 MiB of HBM per device.

```python
import math
import jax
import jax.numpy as jnp
from jax import lax

H = 32
HD = 128
BLOCK = 128
FRAME_BLOCKS = 32
KB = 12
SECTIONS = 4
SEQLEN = 16384
NQB = 128


def block_lists(key):

    def one_section(section):
        sub = jax.random.fold_in(key, 101 + section)
        rows = jnp.arange(NQB, dtype=jnp.int32)
        frame = rows // FRAME_BLOCKS
        noise = jax.random.randint(jax.random.fold_in(sub, 1), (NQB, NQB), 0, 65536, dtype=jnp.int32)
        distinct = noise * NQB + rows[None, :]
        ceiling = 65536 * NQB
        allowed = frame[None, :] <= frame[:, None]
        ranked = jnp.where(rows[None, :] == rows[:, None], 3 * ceiling, jnp.where(allowed, ceiling + distinct, distinct))
        chosen = lax.top_k(ranked, KB)[1].astype(jnp.int32)
        lowest = jnp.minimum(KB, 1 + 3 * frame)
        spread = jax.random.randint(jax.random.fold_in(sub, 2), (NQB,), 0, 65536, dtype=jnp.int32)
        counts = lowest + spread % (KB - lowest + 1)
        counts = counts.at[NQB - 1].set(KB).at[0].set(1)
        return (chosen, counts.astype(jnp.int32))
    return jax.vmap(one_section)(jnp.arange(SECTIONS, dtype=jnp.int32))


def draw_key_blocks(key, part):
    return block_lists(key)[0]


def draw_key_count(key, part):
    return block_lists(key)[1]


def drawn(key):
    shape = (SECTIONS, SEQLEN, H, HD)
    query_full = jnp.clip(jax.random.normal(jax.random.fold_in(key, 31), shape, jnp.float32), -6.0, 6.0)
    key_full = jnp.clip(jax.random.normal(jax.random.fold_in(key, 32), shape, jnp.float32), -6.0, 6.0)
    return (query_full.reshape(SECTIONS, SEQLEN, H * HD).astype(jnp.bfloat16), key_full.reshape(SECTIONS, SEQLEN, H * HD).astype(jnp.bfloat16))


def draw_queries(key, part):
    return drawn(key)[0]


def draw_keys(key, part):
    return drawn(key)[1]


def steps_of(rng, shape, shards, low, top_value):
    def one(dim, parts):
        draws = jax.random.uniform(jax.random.fold_in(jax.random.fold_in(rng, 6), dim), (parts,), jnp.float32, low / len(shards), top_value / len(shards))
        return jnp.repeat(jnp.exp(draws), shape[dim] // parts).reshape((-1,) + (1,) * (len(shape) - dim - 1))

    factor_of = one(*shards[0])
    for cut in shards[1:]:
        factor_of = factor_of * one(*cut)
    return factor_of


def normal_values(rng, dims, width, reach, cuts=(), kind=jnp.bfloat16):
    array = jax.random.normal(rng, dims, jnp.float32) * width
    if len(cuts) > 0:
        array = steps_of(rng, dims, cuts, -0.22, 0.18) * array
    return jnp.clip(array, min=-reach, max=reach).astype(kind)


def setup_inputs(seed: int = 0) -> dict:
    seeds = jax.random.split(jax.random.key(seed), 6)
    return {
        "queries": draw_queries(jax.random.fold_in(seeds[5], 71), 0),
        "keys": draw_keys(jax.random.fold_in(seeds[5], 71), 0),
        "values": normal_values(seeds[2], (SECTIONS, SEQLEN, H * HD), 1.0, 6.0, ((0, 4), (1, 32))),
        "key_blocks": draw_key_blocks(jax.random.fold_in(seeds[5], 71), 0),
        "key_count": draw_key_count(jax.random.fold_in(seeds[5], 71), 0),
    }


def attend_section(queries, keys, values, listed, counted):
    total_blocks = SEQLEN // BLOCK
    scale = 1.0 / math.sqrt(HD)
    query_tiles = queries.reshape(total_blocks, BLOCK, H, HD)
    key_tiles = keys.reshape(total_blocks, BLOCK, H, HD)
    value_tiles = values.reshape(total_blocks, BLOCK, H, HD)
    slots = jnp.arange(KB)

    def one_block(operands):
        query_part, block_ids, count = operands
        near_keys = key_tiles[block_ids].astype(jnp.float32)
        near_values = value_tiles[block_ids].astype(jnp.float32)
        scores = jnp.einsum('rhd,kbhd->hrkb', query_part.astype(jnp.float32), near_keys) * scale
        usable = (slots < count)[None, None, :, None]
        scores = jnp.where(usable, scores, -jnp.inf)
        highest = lax.optimization_barrier(jnp.max(scores, axis=(2, 3), keepdims=True))
        expo = jnp.exp(scores - highest)
        totals = lax.optimization_barrier(jnp.sum(expo, axis=(2, 3)))
        probs = lax.optimization_barrier(expo.astype(jnp.bfloat16)).astype(jnp.float32)
        mixed = jnp.einsum('hrkb,kbhd->rhd', probs, near_values)
        return (mixed / jnp.transpose(totals)[:, :, None]).astype(jnp.bfloat16)
    result = lax.map(one_block, (query_tiles, listed, counted))
    return result.reshape(SEQLEN, H * HD)

def reference(queries, keys, values, key_blocks, key_count):
    outputs = []
    for section in range(SECTIONS):
        outputs.append(attend_section(queries[section], keys[section], values[section], key_blocks[section], key_count[section]))
    stacked = jnp.stack(outputs, axis=0)
    return jnp.roll(stacked, 1, axis=0)
```

```python
import functools
import math

import jax
import jax.numpy as jnp
from jax import lax
from jax.experimental import pallas as pl
from jax.experimental.pallas import tpu as pltpu
from jax.sharding import PartitionSpec as P

HD = 128
BLOCK = 128
KB = 12
SECTIONS = 4
GROUPS = 32
LOCAL = 4
TOKENS = LOCAL * BLOCK
WIDTH = GROUPS * HD
FIRST = 2
SECOND = LOCAL - FIRST
ROWS0 = FIRST * BLOCK
ROWS1 = SECOND * BLOCK
SPAN = 2 * TOKENS + ROWS0
FACTOR = math.log2(math.e) / math.sqrt(HD)
VMEM = 56 * 2**20
BF16 = jnp.bfloat16


def pack_first(q_ref, k_ref, v_ref, o_ref):
    for i in range(o_ref.shape[0]):
        cols = slice(i * HD, (i + 1) * HD)
        o_ref[i, 0:TOKENS] = k_ref[:, cols]
        o_ref[i, TOKENS : 2 * TOKENS] = v_ref[:, cols]
        o_ref[i, 2 * TOKENS : SPAN] = q_ref[:, cols]


def pack_second(q_ref, o_ref):
    for i in range(o_ref.shape[0]):
        o_ref[i] = q_ref[:, i * HD : (i + 1) * HD]


def packed(queries, keys, values):
    per = 4
    wide = pl.BlockSpec((TOKENS, per * HD), lambda i: (0, i))
    first = pl.pallas_call(
        pack_first,
        grid=(GROUPS // per,),
        in_specs=[pl.BlockSpec((ROWS0, per * HD), lambda i: (0, i)), wide, wide],
        out_specs=pl.BlockSpec((per, SPAN, HD), lambda i: (i, 0, 0)),
        out_shape=jax.ShapeDtypeStruct((GROUPS, SPAN, HD), BF16),
        compiler_params=pltpu.CompilerParams(vmem_limit_bytes=VMEM),
    )(queries, keys, values)
    second = pl.pallas_call(
        pack_second,
        grid=(GROUPS // per,),
        in_specs=[pl.BlockSpec((ROWS1, per * HD), lambda i: (ROWS0 // ROWS1, i))],
        out_specs=pl.BlockSpec((per, ROWS1, HD), lambda i: (i, 0, 0)),
        out_shape=jax.ShapeDtypeStruct((GROUPS, ROWS1, HD), BF16),
        compiler_params=pltpu.CompilerParams(vmem_limit_bytes=VMEM),
    )(queries)
    return first, second


def score_tiles(query, count, base, list_ref, kv_ref):
    tiles = []
    for j in range(0, KB, 2):
        near = jnp.concatenate([listed_rows(base, j, 0, list_ref, kv_ref), listed_rows(base, j + 1, 0, list_ref, kv_ref)])
        both = lax.dot_general(query, near, (((1,), (1,)), ((), ())), preferred_element_type=jnp.float32)
        for part, slot in ((both[:, :BLOCK], j), (both[:, BLOCK:], j + 1)):
            tiles.append(jnp.where(slot < count, part, -jnp.inf) if slot else part)
    return tiles


def listed_rows(base, slot, start, list_ref, kv_ref):
    block = list_ref[base + slot]
    row = pl.multiple_of(start + (block % LOCAL) * BLOCK, BLOCK)
    return kv_ref[block // LOCAL, pl.ds(row, BLOCK), :]


def mixed(tiles, highest, base, list_ref, kv_ref):
    total = None
    probs = []
    for tile in tiles:
        expo = jnp.exp2((tile - highest) * FACTOR)
        total = expo if total is None else total + expo
        probs.append(expo.astype(BF16))
    out = None
    for j in range(0, KB, 2):
        near = jnp.concatenate([listed_rows(base, j, TOKENS, list_ref, kv_ref), listed_rows(base, j + 1, TOKENS, list_ref, kv_ref)])
        pair = jnp.concatenate([probs[j], probs[j + 1]], axis=1)
        part = jnp.dot(pair, near, preferred_element_type=jnp.float32)
        out = part if out is None else out + part
    return (out * (1.0 / jnp.sum(total, axis=1, keepdims=True))).astype(BF16)


def attend_blocks(items, list_ref, count_ref, kv_ref):
    for g in range(0, len(items), 2):
        pairs = items[g : g + 2]
        tiles = [score_tiles(query(), count_ref[block], block * KB, list_ref, kv_ref) for block, query, _ in pairs]
        tops = [jnp.max(functools.reduce(jnp.maximum, t), axis=1, keepdims=True) for t in tiles]
        for (block, _, store), t, top in zip(pairs, tiles, tops):
            store(mixed(t, top, block * KB, list_ref, kv_ref))


def attend_first(list_ref, count_ref, kv_ref, o_ref):
    source = pl.program_id(0)
    items = []
    for b in range(FIRST):
        def query(b=b):
            return kv_ref[source, 2 * TOKENS + b * BLOCK : 2 * TOKENS + (b + 1) * BLOCK, :]

        def store(x, b=b):
            o_ref[0, b * BLOCK : (b + 1) * BLOCK, :] = x

        items.append((source * LOCAL + b, query, store))
    attend_blocks(items, list_ref, count_ref, kv_ref)


def attend_second(list_ref, count_ref, side_ref, kv_ref, q_ref, o_ref):
    i = pl.program_id(0)
    source = (i // 4) * 8 + side_ref[0] * 4 + i % 4
    items = []
    for b in range(SECOND):
        def query(b=b):
            return q_ref[0, b * BLOCK : (b + 1) * BLOCK, :]

        def store(x, b=b):
            o_ref[0, b * BLOCK : (b + 1) * BLOCK, :] = x

        items.append((source * LOCAL + FIRST + b, query, store))
    attend_blocks(items, list_ref, count_ref, kv_ref)


def cost(blocks):
    return pl.CostEstimate(
        flops=blocks * KB * BLOCK * BLOCK * HD * 4,
        bytes_accessed=GROUPS * SPAN * HD * 2,
        transcendentals=blocks * KB * BLOCK * BLOCK,
    )


RESIDENT = pl.BlockSpec((GROUPS, SPAN, HD), lambda i, *_: (0, 0, 0), pipeline_mode=pl.Buffered(1))


def first_attention(lists, counts, kv):
    return pl.pallas_call(
        attend_first,
        grid_spec=pltpu.PrefetchScalarGridSpec(
            num_scalar_prefetch=2,
            grid=(GROUPS,),
            in_specs=[RESIDENT],
            out_specs=pl.BlockSpec((1, ROWS0, HD), lambda i, *_: (i, 0, 0)),
        ),
        out_shape=jax.ShapeDtypeStruct((GROUPS, ROWS0, HD), BF16),
        cost_estimate=cost(GROUPS * FIRST),
        compiler_params=pltpu.CompilerParams(vmem_limit_bytes=VMEM),
    )(lists, counts, kv)


def second_attention(lists, counts, side, kv, q):
    return pl.pallas_call(
        attend_second,
        grid_spec=pltpu.PrefetchScalarGridSpec(
            num_scalar_prefetch=3,
            grid=(GROUPS // 2,),
            in_specs=[
                RESIDENT,
                pl.BlockSpec((1, ROWS1, HD), lambda i, l, c, s: ((i // 4) * 8 + s[0] * 4 + i % 4, 0, 0)),
            ],
            out_specs=pl.BlockSpec((1, ROWS1, HD), lambda i, *_: (i, 0, 0)),
        ),
        out_shape=jax.ShapeDtypeStruct((GROUPS // 2, ROWS1, HD), BF16),
        cost_estimate=cost(GROUPS // 2 * SECOND),
        compiler_params=pltpu.CompilerParams(vmem_limit_bytes=VMEM),
    )(lists, counts, side, kv, q)


def unpack(*refs):
    x_ref, o_ref = refs[-2], refs[-1]
    for i in range(x_ref.shape[0]):
        o_ref[:, i * HD : (i + 1) * HD] = x_ref[i]


def unpack_second(s_ref, x_ref, old_ref, o_ref):
    for i in range(x_ref.shape[0]):
        o_ref[:, i * HD : (i + 1) * HD] = x_ref[i]


def unpacked_first(x):
    return pl.pallas_call(
        unpack,
        grid=(GROUPS // 4,),
        in_specs=[pl.BlockSpec((4, ROWS0, HD), lambda i: (i, 0, 0))],
        out_specs=pl.BlockSpec((ROWS0, 4 * HD), lambda i: (0, i)),
        out_shape=jax.ShapeDtypeStruct((TOKENS, WIDTH), BF16),
        compiler_params=pltpu.CompilerParams(vmem_limit_bytes=VMEM),
    )(x)


def unpacked_second(side, x, old):
    return pl.pallas_call(
        unpack_second,
        grid_spec=pltpu.PrefetchScalarGridSpec(
            num_scalar_prefetch=1,
            grid=(GROUPS // 4,),
            in_specs=[
                pl.BlockSpec((4, ROWS1, HD), lambda i, s: (i // 2, (i % 2 + s[0]) % 2, 0)),
                pl.BlockSpec(memory_space=pl.ANY),
            ],
            out_specs=pl.BlockSpec((ROWS1, 4 * HD), lambda i, s: (ROWS0 // ROWS1, i)),
        ),
        out_shape=jax.ShapeDtypeStruct((TOKENS, WIDTH), BF16),
        input_output_aliases={2: 0},
        compiler_params=pltpu.CompilerParams(vmem_limit_bytes=VMEM),
    )(side, x, old)


def handed_on(x, flip):
    def seq(s):
        return s ^ 4 if flip else s

    pairs = [(p * GROUPS + s, (p + 1) % SECTIONS * GROUPS + seq(s)) for p in range(SECTIONS) for s in range(GROUPS)]
    return lax.ppermute(x, ("pipe", "seq"), pairs)


def exchanged(x):
    return lax.all_to_all(x, "seq", split_axis=0, concat_axis=0, tiled=True)


def exchanged_plane(x):
    planes = [[8 * a + 4 * y + z for a in range(4) for z in range(4)] for y in range(2)]
    return lax.all_to_all(x, "seq", split_axis=0, concat_axis=0, tiled=True, axis_index_groups=planes)


def local(queries, keys, values, key_blocks, key_count):
    lists = key_blocks[0].reshape(-1)
    counts = key_count[0]
    side = (lax.axis_index("seq") // 4 % 2).astype(jnp.int32).reshape(1)
    kvq, rest = packed(queries[0], keys[0], values[0])
    kvq = exchanged(kvq)
    rest = exchanged(rest)
    early = handed_on(exchanged(first_attention(lists, counts, kvq)), False)
    near = handed_on(second_attention(lists, counts, side, kvq, rest), False)
    far = handed_on(second_attention(lists, counts, 1 - side, kvq, rest), True)
    late = exchanged_plane(jnp.concatenate([near, far], axis=1))
    return unpacked_second(side, late, unpacked_first(early))[None]


def solution(mesh):
    tokens = P("pipe", "seq", None)
    return jax.shard_map(
        local,
        mesh=mesh,
        in_specs=(tokens, tokens, tokens, P("pipe", None, None), P("pipe", None)),
        out_specs=tokens,
        check_vma=False,
    )
```

```python
import functools
import math

import jax
import jax.numpy as jnp
from jax import lax
from jax.experimental import pallas as pl
from jax.experimental.pallas import tpu as pltpu
from jax.sharding import PartitionSpec as P

HD = 128
BLOCK = 128
KB = 12
SECTIONS = 4
GROUPS = 32
LOCAL = 4
TOKENS = LOCAL * BLOCK
WIDTH = GROUPS * HD
FIRST = 2
SECOND = LOCAL - FIRST
ROWS0 = FIRST * BLOCK
ROWS1 = SECOND * BLOCK
SPAN = 2 * TOKENS + ROWS0
FACTOR = math.log2(math.e) / math.sqrt(HD)
VMEM = 56 * 2**20
BF16 = jnp.bfloat16


def pack(q_ref, k_ref, v_ref, o_ref, rest_ref):
    for i in range(o_ref.shape[0]):
        cols = slice(i * HD, (i + 1) * HD)
        o_ref[i, 0:TOKENS] = k_ref[:, cols]
        o_ref[i, TOKENS : 2 * TOKENS] = v_ref[:, cols]
        o_ref[i, 2 * TOKENS : SPAN] = q_ref[0:ROWS0, cols]
        rest_ref[i] = q_ref[ROWS0:TOKENS, cols]


def packed(queries, keys, values):
    per = 16
    wide = pl.BlockSpec((TOKENS, per * HD), lambda i: (0, i))
    return pl.pallas_call(
        pack,
        grid=(GROUPS // per,),
        in_specs=[wide, wide, wide],
        out_specs=[
            pl.BlockSpec((per, SPAN, HD), lambda i: (i, 0, 0)),
            pl.BlockSpec((per, ROWS1, HD), lambda i: (i, 0, 0)),
        ],
        out_shape=[
            jax.ShapeDtypeStruct((GROUPS, SPAN, HD), BF16),
            jax.ShapeDtypeStruct((GROUPS, ROWS1, HD), BF16),
        ],
        compiler_params=pltpu.CompilerParams(vmem_limit_bytes=VMEM),
    )(queries, keys, values)


def listed_rows(asking, slot, start, list_ref, kv_ref):
    block = list_ref[asking * KB + slot]
    row = pl.multiple_of(start + (block % LOCAL) * BLOCK, BLOCK)
    return kv_ref[block // LOCAL, pl.ds(row, BLOCK), :]


def score_tiles(item, list_ref, count_ref, kv_ref):
    block, load, _ = item
    query, count = load(), count_ref[block]
    tiles = []
    for j in range(0, KB, 2):
        near = jnp.concatenate([listed_rows(block, k, 0, list_ref, kv_ref) for k in (j, j + 1)])
        both = lax.dot_general(query, near, (((1,), (1,)), ((), ())), preferred_element_type=jnp.float32)
        for part, slot in ((both[:, :BLOCK], j), (both[:, BLOCK:], j + 1)):
            tiles.append(jnp.where(slot < count, part, -jnp.inf) if slot else part)
    return tiles


def attend_blocks(items, list_ref, count_ref, kv_ref):
    tiles = score_tiles(items[0], list_ref, count_ref, kv_ref)
    for n, (block, _, store) in enumerate(items):
        highest = jnp.max(functools.reduce(jnp.maximum, tiles), axis=1, keepdims=True)
        ahead = score_tiles(items[n + 1], list_ref, count_ref, kv_ref) if n + 1 < len(items) else None
        total = out = None
        for j in range(0, KB, 2):
            probs = []
            for tile in tiles[j : j + 2]:
                expo = jnp.exp2((tile - highest) * FACTOR)
                total = expo if total is None else total + expo
                probs.append(expo.astype(BF16))
            near = jnp.concatenate([listed_rows(block, k, TOKENS, list_ref, kv_ref) for k in (j, j + 1)])
            part = jnp.dot(jnp.concatenate(probs, axis=1), near, preferred_element_type=jnp.float32)
            out = part if out is None else out + part
        store((out * (1.0 / jnp.sum(total, axis=1, keepdims=True))).astype(BF16))
        tiles = ahead


def attend_first(list_ref, count_ref, kv_ref, o_ref):
    items = []
    for u in range(o_ref.shape[0]):
        source = pl.program_id(0) * o_ref.shape[0] + u
        for b in range(FIRST):
            rows = slice(b * BLOCK, (b + 1) * BLOCK)

            def load(source=source, b=b):
                return kv_ref[source, 2 * TOKENS + b * BLOCK : 2 * TOKENS + (b + 1) * BLOCK, :]

            def store(x, u=u, rows=rows):
                o_ref[u, rows, :] = x

            items.append((source * LOCAL + b, load, store))
    attend_blocks(items, list_ref, count_ref, kv_ref)


def attend_second(list_ref, count_ref, side_ref, kv_ref, q_ref, o_ref):
    items = []
    for u in range(o_ref.shape[0]):
        source = pl.program_id(0) * 8 + side_ref[0] * 4 + u
        for b in range(SECOND):
            rows = slice(b * BLOCK, (b + 1) * BLOCK)

            def load(u=u, rows=rows):
                return q_ref[u, rows, :]

            def store(x, u=u, rows=rows):
                o_ref[u, rows, :] = x

            items.append((source * LOCAL + FIRST + b, load, store))
    attend_blocks(items, list_ref, count_ref, kv_ref)


def cost(blocks):
    return pl.CostEstimate(
        flops=blocks * KB * BLOCK * BLOCK * HD * 4,
        bytes_accessed=GROUPS * SPAN * HD * 2,
        transcendentals=blocks * KB * BLOCK * BLOCK,
    )


def resident(rows):
    return pl.BlockSpec((GROUPS, rows, HD), lambda i, *_: (0, 0, 0), pipeline_mode=pl.Buffered(1))


def first_attention(lists, counts, kv):
    return pl.pallas_call(
        attend_first,
        grid_spec=pltpu.PrefetchScalarGridSpec(
            num_scalar_prefetch=2,
            grid=(GROUPS // 4,),
            in_specs=[resident(SPAN)],
            out_specs=pl.BlockSpec((4, ROWS0, HD), lambda i, *_: (i, 0, 0)),
        ),
        out_shape=jax.ShapeDtypeStruct((GROUPS, ROWS0, HD), BF16),
        cost_estimate=cost(GROUPS * FIRST),
        compiler_params=pltpu.CompilerParams(vmem_limit_bytes=VMEM),
    )(lists, counts, kv)


def second_attention(lists, counts, side, kv, q):
    return pl.pallas_call(
        attend_second,
        grid_spec=pltpu.PrefetchScalarGridSpec(
            num_scalar_prefetch=3,
            grid=(GROUPS // 8,),
            in_specs=[
                resident(2 * TOKENS),
                pl.BlockSpec((4, ROWS1, HD), lambda i, l, c, s: (i * 2 + s[0], 0, 0)),
            ],
            out_specs=pl.BlockSpec((4, ROWS1, HD), lambda i, *_: (i, 0, 0)),
        ),
        out_shape=jax.ShapeDtypeStruct((GROUPS // 2, ROWS1, HD), BF16),
        cost_estimate=cost(GROUPS // 2 * SECOND),
        compiler_params=pltpu.CompilerParams(vmem_limit_bytes=VMEM),
    )(lists, counts, side, kv, q)


def unpack_first(x_ref, o_ref):
    for i in range(x_ref.shape[0]):
        o_ref[:, i * HD : (i + 1) * HD] = x_ref[i]


def unpack_second(side_ref, x_ref, old_ref, o_ref):
    for i in range(x_ref.shape[0]):
        for y in range(2):
            column = (i // 4 * 8 + y * 4 + i % 4) * HD
            row = pl.multiple_of((y ^ side_ref[0]) * ROWS1, ROWS1)
            o_ref[:, column : column + HD] = x_ref[i, pl.ds(row, ROWS1), :]


def unpacked_first(x):
    return pl.pallas_call(
        unpack_first,
        grid=(2,),
        in_specs=[pl.BlockSpec((GROUPS // 2, ROWS0, HD), lambda i: (i, 0, 0))],
        out_specs=pl.BlockSpec((ROWS0, WIDTH // 2), lambda i: (0, i)),
        out_shape=jax.ShapeDtypeStruct((TOKENS, WIDTH), BF16),
        compiler_params=pltpu.CompilerParams(vmem_limit_bytes=VMEM),
    )(x)


def unpacked_second(side, x, old):
    return pl.pallas_call(
        unpack_second,
        grid_spec=pltpu.PrefetchScalarGridSpec(
            num_scalar_prefetch=1,
            grid=(2,),
            in_specs=[
                pl.BlockSpec((GROUPS // 4, 2 * ROWS1, HD), lambda i, s: (i, 0, 0)),
                pl.BlockSpec(memory_space=pl.ANY),
            ],
            out_specs=pl.BlockSpec((ROWS1, WIDTH // 2), lambda i, s: (ROWS0 // ROWS1, i)),
        ),
        out_shape=jax.ShapeDtypeStruct((TOKENS, WIDTH), BF16),
        input_output_aliases={2: 0},
        compiler_params=pltpu.CompilerParams(vmem_limit_bytes=VMEM),
    )(side, x, old)


def handed_on(x, flip):
    def seq(s):
        return s ^ 4 if flip else s

    pairs = [(p * GROUPS + s, (p + 1) % SECTIONS * GROUPS + seq(s)) for p in range(SECTIONS) for s in range(GROUPS)]
    return lax.ppermute(x, ("pipe", "seq"), pairs)


def exchanged(x):
    return lax.all_to_all(x, "seq", split_axis=0, concat_axis=0, tiled=True)


def exchanged_plane(x):
    planes = [[8 * a + 4 * y + z for a in range(4) for z in range(4)] for y in range(2)]
    return lax.all_to_all(x, "seq", split_axis=0, concat_axis=0, tiled=True, axis_index_groups=planes)


def local(queries, keys, values, key_blocks, key_count):
    lists = key_blocks[0].reshape(-1)
    counts = key_count[0]
    side = (lax.axis_index("seq") // 4 % 2).astype(jnp.int32).reshape(1)
    kvq, rest = packed(queries[0], keys[0], values[0])
    kvq, rest, lists, counts, side = lax.optimization_barrier((kvq, rest, lists, counts, side))
    kvq = exchanged(kvq)
    rest = exchanged(rest)
    early = handed_on(exchanged(first_attention(lists, counts, kvq)), False)
    near = handed_on(second_attention(lists, counts, side, kvq, rest), False)
    far = handed_on(second_attention(lists, counts, 1 - side, kvq, rest), True)
    late = exchanged_plane(jnp.concatenate([near, far], axis=1))
    return unpacked_second(side, late, unpacked_first(early))[None]


def solution(mesh):
    tokens = P("pipe", "seq", None)
    return jax.shard_map(
        local,
        mesh=mesh,
        in_specs=(tokens, tokens, tokens, P("pipe", None, None), P("pipe", None)),
        out_specs=tokens,
        check_vma=False,
    )
```

```python
import functools
import math

import jax
import jax.numpy as jnp
from jax import lax
from jax.experimental import pallas as pl
from jax.experimental.pallas import tpu as pltpu
from jax.sharding import PartitionSpec as P

HD = 128
BLOCK = 128
KB = 12
SECTIONS = 4
GROUPS = 32
BLOCKS = 128
LOCAL = 4
TOKENS = LOCAL * BLOCK
WIDTH = GROUPS * HD
HALF = TOKENS // 2
SPAN = 2 * TOKENS + HALF
FACTOR = math.log2(math.e) / math.sqrt(HD)
VMEM = 56 * 2**20
BF16 = jnp.bfloat16


def pack(q_ref, k_ref, v_ref, o_ref, rest_ref):
    for i in range(o_ref.shape[0]):
        cols = slice(i * HD, (i + 1) * HD)
        o_ref[i, 0:TOKENS] = k_ref[:, cols]
        o_ref[i, TOKENS : 2 * TOKENS] = v_ref[:, cols]
        o_ref[i, 2 * TOKENS : SPAN] = q_ref[0:HALF, cols]
        rest_ref[i] = q_ref[HALF:TOKENS, cols]


def packed(queries, keys, values):
    per = 16
    wide = pl.BlockSpec((TOKENS, per * HD), lambda i: (0, i))
    return pl.pallas_call(
        pack,
        grid=(GROUPS // per,),
        in_specs=[wide, wide, wide],
        out_specs=[
            pl.BlockSpec((per, SPAN, HD), lambda i: (i, 0, 0)),
            pl.BlockSpec((per, HALF, HD), lambda i: (i, 0, 0)),
        ],
        out_shape=[
            jax.ShapeDtypeStruct((GROUPS, SPAN, HD), BF16),
            jax.ShapeDtypeStruct((GROUPS, HALF, HD), BF16),
        ],
        compiler_params=pltpu.CompilerParams(vmem_limit_bytes=VMEM),
    )(queries, keys, values)


def listed_rows(asking, slot, start, list_ref, kv_ref):
    block = list_ref[slot * BLOCKS + asking]
    row = pl.multiple_of(start + (block % LOCAL) * BLOCK, BLOCK)
    return kv_ref[block // LOCAL, pl.ds(row, BLOCK), :]


def score_tiles(item, list_ref, count_ref, kv_ref):
    block, load, _ = item
    query, count = load(), count_ref[block]
    tiles = []
    for j in range(0, KB, 2):
        near = jnp.concatenate([listed_rows(block, k, 0, list_ref, kv_ref) for k in (j, j + 1)])
        both = lax.dot_general(query, near, (((1,), (1,)), ((), ())), preferred_element_type=jnp.float32)
        for part, slot in ((both[:, :BLOCK], j), (both[:, BLOCK:], j + 1)):
            tiles.append(jnp.where(slot < count, part, -jnp.inf) if slot else part)
    return tiles


def attend_blocks(items, list_ref, count_ref, kv_ref):
    tiles = score_tiles(items[0], list_ref, count_ref, kv_ref)
    for n, (block, _, store) in enumerate(items):
        highest = jnp.max(functools.reduce(jnp.maximum, tiles), axis=1, keepdims=True)
        ahead = score_tiles(items[n + 1], list_ref, count_ref, kv_ref) if n + 1 < len(items) else None
        total = out = None
        for j in range(0, KB, 2):
            probs = []
            for tile in tiles[j : j + 2]:
                expo = jnp.exp2((tile - highest) * FACTOR)
                total = expo if total is None else total + expo
                probs.append(expo.astype(BF16))
            near = jnp.concatenate([listed_rows(block, k, TOKENS, list_ref, kv_ref) for k in (j, j + 1)])
            part = jnp.dot(jnp.concatenate(probs, axis=1), near, preferred_element_type=jnp.float32)
            out = part if out is None else out + part
        store((out * (1.0 / jnp.sum(total, axis=1, keepdims=True))).astype(BF16))
        tiles = ahead


def attend(first, list_ref, count_ref, side_ref, kv_ref, q_ref, *refs):
    o_ref, mark_ref = refs[-2:]
    mark_ref[...] = jnp.zeros_like(mark_ref)
    items = []
    for u in range(o_ref.shape[0]):
        source = pl.program_id(0) * 8 + (pl.program_id(1) ^ side_ref[0]) * 4 + u
        for b in range(HALF // BLOCK):
            rows = slice(b * BLOCK, (b + 1) * BLOCK)

            def load(u=u, rows=rows):
                return q_ref[u, rows, :]

            def store(x, u=u, rows=rows):
                o_ref[u, rows, :] = x

            items.append((source * LOCAL + first + b, load, store))
    attend_blocks(items, list_ref, count_ref, kv_ref)


def cost(blocks):
    return pl.CostEstimate(
        flops=blocks * KB * BLOCK * BLOCK * HD * 4,
        bytes_accessed=GROUPS * SPAN * HD * 2,
        transcendentals=blocks * KB * BLOCK * BLOCK,
    )


def attention(lists, counts, side, kv, q, first, place, planes, *after):
    return pl.pallas_call(
        functools.partial(attend, first),
        grid_spec=pltpu.PrefetchScalarGridSpec(
            num_scalar_prefetch=3,
            grid=(GROUPS // 8, planes),
            in_specs=[
                pl.BlockSpec((GROUPS, 2 * TOKENS, HD), lambda i, j, *_: (0, 0, 0), pipeline_mode=pl.Buffered(1)),
                pl.BlockSpec((4, HALF, HD), lambda i, j, l, c, s: (i * 2 + (j ^ s[0]), place, 0)),
            ]
            + [pl.BlockSpec(memory_space=pl.ANY)] * len(after),
            out_specs=[
                pl.BlockSpec((4, HALF, HD), lambda i, j, *_: (i, j, 0)),
                pl.BlockSpec((8, HD), lambda i, j, *_: (0, 0)),
            ],
        ),
        out_shape=[
            jax.ShapeDtypeStruct((GROUPS // 2, planes * HALF, HD), BF16),
            jax.ShapeDtypeStruct((8, HD), jnp.float32),
        ],
        cost_estimate=cost(planes * GROUPS // 2 * HALF // BLOCK),
        compiler_params=pltpu.CompilerParams(vmem_limit_bytes=VMEM),
    )(lists, counts, side, kv, q, *after)


def unpack_apart(side_ref, near_ref, far_ref, o_ref):
    for i in range(near_ref.shape[0]):
        for side in range(2):

            @pl.when(side_ref[0] == side)
            def _(i=i, side=side):
                for x_ref, y in ((near_ref, side), (far_ref, 1 - side)):
                    column = (i // 4 * 8 + y * 4 + i % 4) * HD
                    o_ref[:, column : column + HD] = x_ref[i]


def unpack_joined(side_ref, x_ref, old_ref, o_ref):
    for i in range(x_ref.shape[0]):
        for y in range(2):
            column = (i // 4 * 8 + y * 4 + i % 4) * HD
            row = pl.multiple_of((y ^ side_ref[0]) * HALF, HALF)
            o_ref[:, column : column + HD] = x_ref[i, pl.ds(row, HALF), :]


def unpacked(body, side, half, arrived, old):
    blocks = [pl.BlockSpec((GROUPS // 4, x.shape[1], HD), lambda i, s: (i, 0, 0)) for x in arrived]
    return pl.pallas_call(
        body,
        grid_spec=pltpu.PrefetchScalarGridSpec(
            num_scalar_prefetch=1,
            grid=(2,),
            in_specs=blocks + [pl.BlockSpec(memory_space=pl.ANY)] * len(old),
            out_specs=pl.BlockSpec((HALF, WIDTH // 2), lambda i, s: (half, i)),
        ),
        out_shape=jax.ShapeDtypeStruct((TOKENS, WIDTH), BF16),
        input_output_aliases={2: 0} if old else {},
        compiler_params=pltpu.CompilerParams(vmem_limit_bytes=VMEM),
    )(side, *arrived, *old)


def fill(x_ref, *refs):
    refs[-1][...] = x_ref[...]


def joined(half, x, old):
    return pl.pallas_call(
        fill,
        grid=(2,),
        in_specs=[pl.BlockSpec((GROUPS // 4, HALF, HD), lambda i: (i, 0, 0))]
        + [pl.BlockSpec(memory_space=pl.ANY)] * len(old),
        out_specs=pl.BlockSpec((GROUPS // 4, HALF, HD), lambda i: (i, half, 0)),
        out_shape=jax.ShapeDtypeStruct((GROUPS // 2, 2 * HALF, HD), BF16),
        input_output_aliases={1: 0} if old else {},
        cost_estimate=pl.CostEstimate(flops=4 * 10**9, bytes_accessed=2 * x.size * 2, transcendentals=0),
        compiler_params=pltpu.CompilerParams(vmem_limit_bytes=VMEM),
    )(x, *old)


def handed_on(x, flip):
    def seq(s):
        return s ^ 4 if flip else s

    pairs = [(p * GROUPS + s, (p + 1) % SECTIONS * GROUPS + seq(s)) for p in range(SECTIONS) for s in range(GROUPS)]
    return lax.ppermute(x, ("pipe", "seq"), pairs)


def exchanged(x):
    return lax.all_to_all(x, "seq", split_axis=0, concat_axis=0, tiled=True)


def exchanged_plane(x):
    planes = [[8 * a + 4 * y + z for a in range(4) for z in range(4)] for y in range(2)]
    return lax.all_to_all(x, "seq", split_axis=0, concat_axis=0, tiled=True, axis_index_groups=planes)


def local(queries, keys, values, key_blocks, key_count):
    lists = key_blocks[0].T.reshape(-1)
    counts = key_count[0]
    side = (lax.axis_index("seq") // 4 % 2).astype(jnp.int32).reshape(1)
    kvq, rest = packed(queries[0], keys[0], values[0])
    kvq, rest, lists, counts, side = lax.optimization_barrier((kvq, rest, lists, counts, side))
    kvq = exchanged(kvq)
    rest = exchanged(rest)
    early = exchanged_plane(attention(lists, counts, side, kvq, kvq, 0, 2 * TOKENS // HALF, 2)[0])
    far, mark = attention(lists, counts, 1 - side, kvq, rest, HALF // BLOCK, 0, 1)
    near, _ = attention(lists, counts, side, kvq, rest, HALF // BLOCK, 0, 1, mark)
    late = joined(0, handed_on(near, False), (joined(1, handed_on(far, True), ()),))
    early, late = lax.optimization_barrier((early, late))
    late = exchanged_plane(late)
    early = handed_on(early[:, :HALF], False), handed_on(early[:, HALF:], True)
    out = unpacked(unpack_apart, side, 0, early, ())
    return unpacked(unpack_joined, side, 1, (late,), (out,))[None]


def solution(mesh):
    tokens = P("pipe", "seq", None)
    return jax.shard_map(
        local,
        mesh=mesh,
        in_specs=(tokens, tokens, tokens, P("pipe", None, None), P("pipe", None)),
        out_specs=tokens,
        check_vma=False,
    )
```

```python
import functools
import math

import jax
import jax.numpy as jnp
from jax import lax
from jax.experimental import pallas as pl
from jax.experimental.pallas import tpu as pltpu
from jax.sharding import PartitionSpec as P

HD = 128
BLOCK = 128
KB = 12
SECTIONS = 4
GROUPS = 32
BLOCKS = 128
LOCAL = 4
TOKENS = LOCAL * BLOCK
WIDTH = GROUPS * HD
HALF = TOKENS // 2
SPAN = 2 * TOKENS + HALF
FACTOR = math.log2(math.e) / math.sqrt(HD)
VMEM = 56 * 2**20
BF16 = jnp.bfloat16


def pack(q_ref, k_ref, v_ref, o_ref, rest_ref):
    for i in range(rest_ref.shape[0]):
        cols = slice(i * HD, (i + 1) * HD)
        head = pl.program_id(0) * rest_ref.shape[0] + i
        o_ref[head, 0:TOKENS] = k_ref[:, cols]
        o_ref[head, TOKENS : 2 * TOKENS] = v_ref[:, cols]
        o_ref[head, 2 * TOKENS : SPAN] = q_ref[0:HALF, cols]
        rest_ref[i] = q_ref[HALF:TOKENS, cols]


def packed(queries, keys, values):
    per = 8
    wide = pl.BlockSpec((TOKENS, per * HD), lambda i: (0, i))
    return pl.pallas_call(
        pack,
        grid=(GROUPS // per,),
        in_specs=[wide, wide, wide],
        out_specs=[
            pl.BlockSpec(memory_space=pltpu.VMEM),
            pl.BlockSpec((per, HALF, HD), lambda i: (i, 0, 0)),
        ],
        out_shape=[
            pltpu.VMEM((GROUPS, SPAN, HD), BF16),
            jax.ShapeDtypeStruct((GROUPS, HALF, HD), BF16),
        ],
        compiler_params=pltpu.CompilerParams(vmem_limit_bytes=40 * 2**20),
    )(queries, keys, values)


def listed_rows(asking, slot, start, list_ref, kv_ref):
    block = list_ref[slot * BLOCKS + asking]
    row = pl.multiple_of(start + (block % LOCAL) * BLOCK, BLOCK)
    return kv_ref[block // LOCAL, pl.ds(row, BLOCK), :]


def score_tiles(item, list_ref, count_ref, kv_ref):
    block, load, _ = item
    query, count = load(), count_ref[block]
    tiles = []
    for j in range(0, KB, 2):
        near = jnp.concatenate([listed_rows(block, k, 0, list_ref, kv_ref) for k in (j, j + 1)])
        both = lax.dot_general(query, near, (((1,), (1,)), ((), ())), preferred_element_type=jnp.float32)
        for part, slot in ((both[:, :BLOCK], j), (both[:, BLOCK:], j + 1)):
            tiles.append(jnp.where(slot < count, part, -jnp.inf) if slot else part)
    return tiles


def attend_blocks(items, list_ref, count_ref, kv_ref):
    tiles = score_tiles(items[0], list_ref, count_ref, kv_ref)
    for n, (block, _, store) in enumerate(items):
        highest = jnp.max(functools.reduce(jnp.maximum, tiles), axis=1, keepdims=True)
        ahead = score_tiles(items[n + 1], list_ref, count_ref, kv_ref) if n + 1 < len(items) else None
        total = out = None
        for j in range(0, KB, 2):
            probs = []
            for tile in tiles[j : j + 2]:
                expo = jnp.exp2((tile - highest) * FACTOR)
                total = expo if total is None else total + expo
                probs.append(expo.astype(BF16))
            near = jnp.concatenate([listed_rows(block, k, TOKENS, list_ref, kv_ref) for k in (j, j + 1)])
            part = jnp.dot(jnp.concatenate(probs, axis=1), near, preferred_element_type=jnp.float32)
            out = part if out is None else out + part
        store((out * (1.0 / jnp.sum(total, axis=1, keepdims=True))).astype(BF16))
        tiles = ahead


def attend(first, list_ref, count_ref, side_ref, kv_ref, q_ref, *refs):
    o_ref, mark_ref = refs[-2:]
    mark_ref[...] = jnp.zeros_like(mark_ref)
    items = []
    for u in range(o_ref.shape[0]):
        source = pl.program_id(0) * 8 + (pl.program_id(1) ^ side_ref[0]) * 4 + u
        for b in range(HALF // BLOCK):
            rows = slice(b * BLOCK, (b + 1) * BLOCK)

            def load(u=u, rows=rows):
                return q_ref[u, rows, :]

            def store(x, u=u, rows=rows):
                o_ref[u, rows, :] = x

            items.append((source * LOCAL + first + b, load, store))
    attend_blocks(items, list_ref, count_ref, kv_ref)


def cost(blocks):
    return pl.CostEstimate(
        flops=blocks * KB * BLOCK * BLOCK * HD * 4,
        bytes_accessed=GROUPS * SPAN * HD * 2,
        transcendentals=blocks * KB * BLOCK * BLOCK,
    )


def attention(lists, counts, side, kv, q, first, place, planes, *after):
    return pl.pallas_call(
        functools.partial(attend, first),
        grid_spec=pltpu.PrefetchScalarGridSpec(
            num_scalar_prefetch=3,
            grid=(GROUPS // 8, planes),
            in_specs=[
                pl.BlockSpec((GROUPS, 2 * TOKENS, HD), lambda i, j, *_: (0, 0, 0), pipeline_mode=pl.Buffered(1)),
                pl.BlockSpec((4, HALF, HD), lambda i, j, l, c, s: (i * 2 + (j ^ s[0]), place, 0)),
            ]
            + [pl.BlockSpec(memory_space=pl.ANY)] * len(after),
            out_specs=[
                pl.BlockSpec((4, HALF, HD), lambda i, j, *_: (i, j, 0)),
                pl.BlockSpec((8, HD), lambda i, j, *_: (0, 0)),
            ],
        ),
        out_shape=[
            jax.ShapeDtypeStruct((GROUPS // 2, planes * HALF, HD), BF16),
            jax.ShapeDtypeStruct((8, HD), jnp.float32),
        ],
        cost_estimate=cost(planes * GROUPS // 2 * HALF // BLOCK),
        compiler_params=pltpu.CompilerParams(vmem_limit_bytes=VMEM),
    )(lists, counts, side, kv, q, *after)


def unpack_apart(side_ref, near_ref, far_ref, o_ref):
    for i in range(near_ref.shape[0]):
        for side in range(2):

            @pl.when(side_ref[0] == side)
            def _(i=i, side=side):
                for x_ref, y in ((near_ref, side), (far_ref, 1 - side)):
                    column = (i // 4 * 8 + y * 4 + i % 4) * HD
                    o_ref[:, column : column + HD] = x_ref[i]


def unpack_last(side_ref, x_ref, old_ref, o_ref, sem):
    copies = []
    for i in range(x_ref.shape[0]):
        for y in range(2):
            column = (i // 4 * 8 + y * 4 + i % 4) * HD
            row = pl.multiple_of((y ^ side_ref[0]) * HALF, HALF)
            copies.append(
                pltpu.make_async_copy(
                    x_ref.at[i, pl.ds(row, HALF)],
                    o_ref.at[HALF:TOKENS, column : column + HD],
                    sem.at[2 * i + y],
                )
            )
    for copy in copies:
        copy.start()
    for copy in copies:
        copy.wait()


def unpacked_last(side, x, old):
    anywhere = pl.BlockSpec(memory_space=pl.ANY)
    return pl.pallas_call(
        unpack_last,
        in_specs=[pl.BlockSpec(memory_space=pltpu.SMEM), pl.BlockSpec(memory_space=pltpu.VMEM), anywhere],
        out_specs=anywhere,
        out_shape=jax.ShapeDtypeStruct((TOKENS, WIDTH), BF16),
        scratch_shapes=[pltpu.SemaphoreType.DMA((GROUPS,))],
        input_output_aliases={2: 0},
        cost_estimate=pl.CostEstimate(flops=10**9, bytes_accessed=4 * HALF * WIDTH, transcendentals=0),
        compiler_params=pltpu.CompilerParams(vmem_limit_bytes=16 * 2**20),
    )(side, held(x), old)


def unpacked(body, side, half, arrived, old):
    blocks = [pl.BlockSpec((GROUPS // 4, x.shape[1], HD), lambda i, s: (i, 0, 0)) for x in arrived]
    return pl.pallas_call(
        body,
        grid_spec=pltpu.PrefetchScalarGridSpec(
            num_scalar_prefetch=1,
            grid=(2,),
            in_specs=blocks + [pl.BlockSpec(memory_space=pl.ANY)] * len(old),
            out_specs=pl.BlockSpec((HALF, WIDTH // 2), lambda i, s: (half, i)),
        ),
        out_shape=jax.ShapeDtypeStruct((TOKENS, WIDTH), BF16),
        input_output_aliases={2: 0} if old else {},
        cost_estimate=pl.CostEstimate(flops=(1 if old else 60) * 10**9, bytes_accessed=4 * HALF * WIDTH, transcendentals=0),
        compiler_params=pltpu.CompilerParams(vmem_limit_bytes=VMEM),
    )(side, *arrived, *old)


def cut(x_ref, mark_ref, near_ref, far_ref):
    near_ref[...] = x_ref[:, :HALF]
    far_ref[...] = x_ref[:, HALF:]


def split(x, after):
    part = pl.BlockSpec((GROUPS // 4, HALF, HD), lambda i: (i, 0, 0))
    shape = jax.ShapeDtypeStruct((GROUPS // 2, HALF, HD), BF16)
    return pl.pallas_call(
        cut,
        grid=(2,),
        in_specs=[
            pl.BlockSpec((GROUPS // 4, 2 * HALF, HD), lambda i: (i, 0, 0)),
            pl.BlockSpec(memory_space=pl.ANY),
        ],
        out_specs=[part, part],
        out_shape=[shape, shape],
        compiler_params=pltpu.CompilerParams(vmem_limit_bytes=VMEM),
    )(x, after)


def held(x):
    return pltpu.with_memory_space_constraint(x, pltpu.VMEM)


def fill(half, x_ref, *refs):
    o_ref, sem = refs[-2:]
    copy = pltpu.make_async_copy(x_ref, o_ref.at[:, half * HALF : (half + 1) * HALF], sem)
    copy.start()
    copy.wait()


def joined(half, x, old, cover=10**9):
    return pl.pallas_call(
        functools.partial(fill, half),
        in_specs=[pl.BlockSpec(memory_space=pltpu.VMEM)] + [pl.BlockSpec(memory_space=pl.ANY)] * len(old),
        out_specs=pl.BlockSpec(memory_space=pl.ANY),
        out_shape=jax.ShapeDtypeStruct((GROUPS // 2, 2 * HALF, HD), BF16),
        scratch_shapes=[pltpu.SemaphoreType.DMA],
        input_output_aliases={1: 0} if old else {},
        cost_estimate=pl.CostEstimate(flops=cover, bytes_accessed=2 * x.size * 2, transcendentals=0),
        compiler_params=pltpu.CompilerParams(vmem_limit_bytes=16 * 2**20),
    )(held(x), *old)


def handed_on(x, flip):
    def seq(s):
        return s ^ 4 if flip else s

    pairs = [(p * GROUPS + s, (p + 1) % SECTIONS * GROUPS + seq(s)) for p in range(SECTIONS) for s in range(GROUPS)]
    return lax.ppermute(x, ("pipe", "seq"), pairs)


def exchanged(x):
    return lax.all_to_all(x, "seq", split_axis=0, concat_axis=0, tiled=True)


def exchanged_plane(x):
    planes = [[8 * a + 4 * y + z for a in range(4) for z in range(4)] for y in range(2)]
    return lax.all_to_all(x, "seq", split_axis=0, concat_axis=0, tiled=True, axis_index_groups=planes)


def local(queries, keys, values, key_blocks, key_count):
    side = (lax.axis_index("seq") // 4 % 2).astype(jnp.int32).reshape(1)
    kvq, rest = packed(queries[0], keys[0], values[0])
    kvq, rest, side = lax.optimization_barrier((kvq, rest, side))
    kvq, rest, key_blocks, key_count = lax.optimization_barrier((exchanged(kvq), rest, key_blocks, key_count))
    lists = key_blocks[0].T.reshape(-1)
    counts = key_count[0]
    rest = exchanged(rest)
    early = exchanged_plane(attention(lists, counts, side, kvq, kvq, 0, 2 * TOKENS // HALF, 2)[0])
    far, mark = attention(lists, counts, 1 - side, kvq, rest, HALF // BLOCK, 0, 1)
    near, mark = attention(lists, counts, side, kvq, rest, HALF // BLOCK, 0, 1, mark)
    late = joined(1, handed_on(far, True), (), 20 * 10**9)
    early = split(early, mark)
    early, near, late = lax.optimization_barrier((early, handed_on(near, False), late))
    late = exchanged_plane(joined(0, near, (late,)))
    early = handed_on(early[0], False), handed_on(early[1], True)
    out = unpacked(unpack_apart, side, 0, early, ())
    return unpacked_last(side, late, out)[None]


def solution(mesh):
    tokens = P("pipe", "seq", None)
    return jax.shard_map(
        local,
        mesh=mesh,
        in_specs=(tokens, tokens, tokens, P("pipe", None, None), P("pipe", None)),
        out_specs=tokens,
        check_vma=False,
    )
```

```python
import functools
import math

import jax
import jax.numpy as jnp
from jax import lax
from jax.experimental import pallas as pl
from jax.experimental.pallas import tpu as pltpu
from jax.sharding import PartitionSpec as P

HD = 128
BLOCK = 128
KB = 12
SECTIONS = 4
GROUPS = 32
BLOCKS = 128
LOCAL = 4
TOKENS = LOCAL * BLOCK
WIDTH = GROUPS * HD
HALF = TOKENS // 2
SPAN = 2 * TOKENS + HALF
FACTOR = math.log2(math.e) / math.sqrt(HD)
VMEM = 56 * 2**20
BF16 = jnp.bfloat16


def pack(q_ref, k_ref, v_ref, o_ref, rest_ref):
    for i in range(rest_ref.shape[0]):
        cols = slice(i * HD, (i + 1) * HD)
        head = pl.program_id(0) * rest_ref.shape[0] + i
        o_ref[head, 0:TOKENS] = k_ref[:, cols]
        o_ref[head, TOKENS : 2 * TOKENS] = v_ref[:, cols]
        o_ref[head, 2 * TOKENS : SPAN] = q_ref[0:HALF, cols]
        rest_ref[i] = q_ref[HALF:TOKENS, cols]


def packed(queries, keys, values):
    per = 16
    wide = pl.BlockSpec((TOKENS, per * HD), lambda i: (0, i))
    return pl.pallas_call(
        pack,
        grid=(GROUPS // per,),
        in_specs=[wide, wide, wide],
        out_specs=[
            pl.BlockSpec(memory_space=pltpu.VMEM),
            pl.BlockSpec((per, HALF, HD), lambda i: (i, 0, 0)),
        ],
        out_shape=[
            pltpu.VMEM((GROUPS, SPAN, HD), BF16),
            jax.ShapeDtypeStruct((GROUPS, HALF, HD), BF16),
        ],
        compiler_params=pltpu.CompilerParams(vmem_limit_bytes=40 * 2**20),
    )(queries, keys, values)


def listed_rows(asking, slot, start, list_ref, kv_ref):
    block = list_ref[slot * BLOCKS + asking]
    row = pl.multiple_of(start + (block % LOCAL) * BLOCK, BLOCK)
    return kv_ref[block // LOCAL, pl.ds(row, BLOCK), :]


def score_tiles(item, list_ref, count_ref, kv_ref):
    block, load, _ = item
    query, count = load(), count_ref[block]
    tiles = []
    for j in range(0, KB, 2):
        near = jnp.concatenate([listed_rows(block, k, 0, list_ref, kv_ref) for k in (j, j + 1)])
        both = lax.dot_general(query, near, (((1,), (1,)), ((), ())), preferred_element_type=jnp.float32)
        for part, slot in ((both[:, :BLOCK], j), (both[:, BLOCK:], j + 1)):
            tiles.append(jnp.where(slot < count, part, -jnp.inf) if slot else part)
    return tiles


def attend_blocks(items, list_ref, count_ref, kv_ref):
    tiles = score_tiles(items[0], list_ref, count_ref, kv_ref)
    for n, (block, _, store) in enumerate(items):
        highest = jnp.max(functools.reduce(jnp.maximum, tiles), axis=1, keepdims=True)
        ahead = score_tiles(items[n + 1], list_ref, count_ref, kv_ref) if n + 1 < len(items) else None
        total = out = None
        for j in range(0, KB, 2):
            probs = []
            for tile in tiles[j : j + 2]:
                expo = jnp.exp2((tile - highest) * FACTOR)
                total = expo if total is None else total + expo
                probs.append(expo.astype(BF16))
            near = jnp.concatenate([listed_rows(block, k, TOKENS, list_ref, kv_ref) for k in (j, j + 1)])
            part = jnp.dot(jnp.concatenate(probs, axis=1), near, preferred_element_type=jnp.float32)
            out = part if out is None else out + part
        store((out * (1.0 / jnp.sum(total, axis=1, keepdims=True))).astype(BF16))
        tiles = ahead


def attend(first, list_ref, count_ref, side_ref, kv_ref, q_ref, *refs):
    o_ref, mark_ref = refs[-2:]
    mark_ref[...] = jnp.zeros_like(mark_ref)
    items = []
    for u in range(o_ref.shape[0]):
        source = pl.program_id(0) * 8 + (pl.program_id(1) ^ side_ref[0]) * 4 + u
        for b in range(HALF // BLOCK):
            rows = slice(b * BLOCK, (b + 1) * BLOCK)

            def load(u=u, rows=rows):
                return q_ref[u, rows, :]

            def store(x, u=u, rows=rows):
                o_ref[u, rows, :] = x

            items.append((source * LOCAL + first + b, load, store))
    attend_blocks(items, list_ref, count_ref, kv_ref)


def cost(blocks):
    return pl.CostEstimate(
        flops=blocks * KB * BLOCK * BLOCK * HD * 4,
        bytes_accessed=GROUPS * SPAN * HD * 2,
        transcendentals=blocks * KB * BLOCK * BLOCK,
    )


def attention(lists, counts, side, kv, q, first, place, planes, *after):
    return pl.pallas_call(
        functools.partial(attend, first),
        grid_spec=pltpu.PrefetchScalarGridSpec(
            num_scalar_prefetch=3,
            grid=(GROUPS // 8, planes),
            in_specs=[
                pl.BlockSpec((GROUPS, 2 * TOKENS, HD), lambda i, j, *_: (0, 0, 0), pipeline_mode=pl.Buffered(1)),
                pl.BlockSpec((4, HALF, HD), lambda i, j, l, c, s: (i * 2 + (j ^ s[0]), place, 0)),
            ]
            + [pl.BlockSpec(memory_space=pl.ANY)] * len(after),
            out_specs=[
                pl.BlockSpec((4, HALF, HD), lambda i, j, *_: (i, j, 0)),
                pl.BlockSpec((8, HD), lambda i, j, *_: (0, 0)),
            ],
        ),
        out_shape=[
            jax.ShapeDtypeStruct((GROUPS // 2, planes * HALF, HD), BF16),
            jax.ShapeDtypeStruct((8, HD), jnp.float32),
        ],
        cost_estimate=cost(planes * GROUPS // 2 * HALF // BLOCK),
        compiler_params=pltpu.CompilerParams(vmem_limit_bytes=VMEM),
    )(lists, counts, side, kv, q, *after)


def unpack_apart(side_ref, near_ref, far_ref, o_ref):
    for i in range(near_ref.shape[0]):
        for side in range(2):

            @pl.when(side_ref[0] == side)
            def _(i=i, side=side):
                for x_ref, y in ((near_ref, side), (far_ref, 1 - side)):
                    column = (i // 4 * 8 + y * 4 + i % 4) * HD
                    o_ref[:, column : column + HD] = x_ref[i]


def unpack_last(side_ref, x_ref, old_ref, o_ref, sem):
    copies = []
    for i in range(x_ref.shape[0]):
        for y in range(2):
            column = (i // 4 * 8 + y * 4 + i % 4) * HD
            row = pl.multiple_of((y ^ side_ref[0]) * HALF, HALF)
            copies.append(
                pltpu.make_async_copy(
                    x_ref.at[i, pl.ds(row, HALF)],
                    o_ref.at[HALF:TOKENS, column : column + HD],
                    sem.at[2 * i + y],
                )
            )
    for copy in copies:
        copy.start()
    for copy in copies:
        copy.wait()


def unpacked_last(side, x, old):
    anywhere = pl.BlockSpec(memory_space=pl.ANY)
    return pl.pallas_call(
        unpack_last,
        in_specs=[pl.BlockSpec(memory_space=pltpu.SMEM), pl.BlockSpec(memory_space=pltpu.VMEM), anywhere],
        out_specs=anywhere,
        out_shape=jax.ShapeDtypeStruct((TOKENS, WIDTH), BF16),
        scratch_shapes=[pltpu.SemaphoreType.DMA((GROUPS,))],
        input_output_aliases={2: 0},
        cost_estimate=pl.CostEstimate(flops=10**9, bytes_accessed=4 * HALF * WIDTH, transcendentals=0),
        compiler_params=pltpu.CompilerParams(vmem_limit_bytes=16 * 2**20),
    )(side, held(x), old)


def unpacked(body, side, half, arrived, old):
    blocks = [pl.BlockSpec((GROUPS // 4, x.shape[1], HD), lambda i, s: (i, 0, 0)) for x in arrived]
    return pl.pallas_call(
        body,
        grid_spec=pltpu.PrefetchScalarGridSpec(
            num_scalar_prefetch=1,
            grid=(2,),
            in_specs=blocks + [pl.BlockSpec(memory_space=pl.ANY)] * len(old),
            out_specs=pl.BlockSpec((HALF, WIDTH // 2), lambda i, s: (half, i)),
        ),
        out_shape=jax.ShapeDtypeStruct((TOKENS, WIDTH), BF16),
        input_output_aliases={2: 0} if old else {},
        cost_estimate=pl.CostEstimate(flops=(1 if old else 60) * 10**9, bytes_accessed=4 * HALF * WIDTH, transcendentals=0),
        compiler_params=pltpu.CompilerParams(vmem_limit_bytes=VMEM),
    )(side, *arrived, *old)


def cut(x_ref, mark_ref, near_ref, far_ref):
    near_ref[...] = x_ref[:, :HALF]
    far_ref[...] = x_ref[:, HALF:]


def split(x, after):
    part = pl.BlockSpec((GROUPS // 4, HALF, HD), lambda i: (i, 0, 0))
    shape = jax.ShapeDtypeStruct((GROUPS // 2, HALF, HD), BF16)
    return pl.pallas_call(
        cut,
        grid=(2,),
        in_specs=[
            pl.BlockSpec((GROUPS // 4, 2 * HALF, HD), lambda i: (i, 0, 0)),
            pl.BlockSpec(memory_space=pl.ANY),
        ],
        out_specs=[part, part],
        out_shape=[shape, shape],
        compiler_params=pltpu.CompilerParams(vmem_limit_bytes=VMEM),
    )(x, after)


def held(x):
    return pltpu.with_memory_space_constraint(x, pltpu.VMEM)


def fill(half, x_ref, *refs):
    o_ref, sem = refs[-2:]
    copy = pltpu.make_async_copy(x_ref, o_ref.at[:, half * HALF : (half + 1) * HALF], sem)
    copy.start()
    copy.wait()


def joined(half, x, old, cover=10**9):
    return pl.pallas_call(
        functools.partial(fill, half),
        in_specs=[pl.BlockSpec(memory_space=pltpu.VMEM)] + [pl.BlockSpec(memory_space=pl.ANY)] * len(old),
        out_specs=pl.BlockSpec(memory_space=pl.ANY),
        out_shape=jax.ShapeDtypeStruct((GROUPS // 2, 2 * HALF, HD), BF16),
        scratch_shapes=[pltpu.SemaphoreType.DMA],
        input_output_aliases={1: 0} if old else {},
        cost_estimate=pl.CostEstimate(flops=cover, bytes_accessed=2 * x.size * 2, transcendentals=0),
        compiler_params=pltpu.CompilerParams(vmem_limit_bytes=16 * 2**20),
    )(held(x), *old)


def handed_on(x, flip):
    def seq(s):
        return s ^ 4 if flip else s

    pairs = [(p * GROUPS + s, (p + 1) % SECTIONS * GROUPS + seq(s)) for p in range(SECTIONS) for s in range(GROUPS)]
    return lax.ppermute(x, ("pipe", "seq"), pairs)


def exchanged(x):
    return lax.all_to_all(x, "seq", split_axis=0, concat_axis=0, tiled=True)


def exchanged_plane(x):
    planes = [[8 * a + 4 * y + z for a in range(4) for z in range(4)] for y in range(2)]
    return lax.all_to_all(x, "seq", split_axis=0, concat_axis=0, tiled=True, axis_index_groups=planes)


def local(queries, keys, values, key_blocks, key_count):
    side = (lax.axis_index("seq") // 4 % 2).astype(jnp.int32).reshape(1)
    kvq, rest = packed(queries[0], keys[0], values[0])
    kvq, rest, side = lax.optimization_barrier((kvq, rest, side))
    kvq, rest, key_blocks, key_count = lax.optimization_barrier((exchanged(kvq), rest, key_blocks, key_count))
    lists = key_blocks[0].T.reshape(-1)
    counts = key_count[0]
    rest = exchanged(rest)
    early = exchanged_plane(attention(lists, counts, side, kvq, kvq, 0, 2 * TOKENS // HALF, 2)[0])
    far, mark = attention(lists, counts, 1 - side, kvq, rest, HALF // BLOCK, 0, 1)
    near, mark = attention(lists, counts, side, kvq, rest, HALF // BLOCK, 0, 1, mark)
    late = joined(1, handed_on(far, True), (), 20 * 10**9)
    early = split(early, mark)
    early, near, late = lax.optimization_barrier((early, handed_on(near, False), late))
    late = exchanged_plane(joined(0, near, (late,)))
    early = handed_on(early[0], False), handed_on(early[1], True)
    out = unpacked(unpack_apart, side, 0, early, ())
    return unpacked_last(side, late, out)[None]


def solution(mesh):
    tokens = P("pipe", "seq", None)
    return jax.shard_map(
        local,
        mesh=mesh,
        in_specs=(tokens, tokens, tokens, P("pipe", None, None), P("pipe", None)),
        out_specs=tokens,
        check_vma=False,
    )
```
